256 devices in a mesh: dp: 8 (over z), pipe: 4 (over y), seq: 8 (over x, core).
Axes of the slice: x: 4, y: 4, z: 8, core: 2. Of those that a mesh axis runs over, the one named last changes fastest.
Arguments:
- section_input: bfloat16 [4, 8, 1024, 1024], P('pipe', 'dp', 'seq'), may hold values from -6 to 6
- event_ids: int32 [8, 1024], P('dp', 'seq'), may hold values from 0 to 63
- lengths: int32 [8], P('dp'), may hold values from 256 to 1024, as said below
- clicks: int32 [8, 1024], P('dp', 'seq'), may hold values 0 or 1
- conversions: int32 [8, 1024], P('dp', 'seq'), may hold values 0 or 1
- conv_weight: bfloat16 [4, 3072, 1024], P('pipe'), may hold values from -0.109375 to 0.109375
- type_table: bfloat16 [4, 64, 1024], P('pipe'), may hold values from -3 to 3
- head_weight: bfloat16 [2, 1024], replicated, may hold values from -0.375 to 0.375
Outputs:
- conv_grad: float32 [4, 3072, 1024], P('pipe', ('dp', 'seq'))
- type_grad: float32 [4, 64, 1024], P('pipe', ('dp', 'seq'))
- input_grad: bfloat16 [4, 8, 1024, 1024], P('pipe', 'dp', 'seq')
The draws below stay inside these ranges and needn't reach their ends.
Inputs may be any that keep to these rules, and one draw needn't show every extreme that they name: `lengths`: some history has all 1024 events real.
All inputs are finite; a program needn't handle non-finite values. No bound on the sum of `clicks` or of `conversions` on one device may be relied on, other than what follows from the above.
Results may differ from the reference program's by a relative error of at most 0.013.
Values may be sent and summed in bfloat16 or wider, within the bound.
No kernel may reach another device: no remote copies, remote signals or barrier semaphores. Data moves between devices by JAX's collectives and lax.ppermute only.
A program may use at most 256 MiB of HBM per device.

```python
import math
import jax
import jax.numpy as jnp
import numpy as np
from jax import lax

D = 1024
TYPES = 64
KERNEL = 3
S_DEV = 128
SEQ = 1024
LAYERS = 4
USERS = 8
N_PIPE = 4


def draw_lengths(key, part):
    key_len = jax.random.fold_in(key, 11)
    key_pick = jax.random.fold_in(key, 12)
    drawn = SEQ // 4 + jax.random.randint(key_len, (USERS,), 0, SEQ - SEQ // 4 + 1, dtype=jnp.int32)
    chosen = jax.random.randint(key_pick, (), 0, USERS, dtype=jnp.int32)
    return jnp.where(jnp.arange(USERS, dtype=jnp.int32) == chosen, jnp.int32(SEQ), drawn).astype(jnp.int32)


def plant(array, stream_key, low, high):
    spot = [jax.random.randint(jax.random.fold_in(stream_key, axis), (), 0, length) for axis, length in enumerate(array.shape)]
    widest = array.shape.index(max(array.shape))
    next_to = spot[:widest] + [(spot[widest] + 1) % array.shape[widest]] + spot[widest + 1:]
    return array.at[tuple(spot)].set(low).at[tuple(next_to)].set(high)


def block_scale(stream_key, extent, shards, least, high):
    gain, own = 1.0, jax.random.fold_in(stream_key, 6)
    for dim, shards_of in shards:
        draws = jnp.exp(jax.random.uniform(jax.random.fold_in(own, dim), (shards_of,), jnp.float32, least / len(shards), high / len(shards)))
        gain = gain * jnp.repeat(draws, extent[dim] // shards_of).reshape([-1 if axis == dim else 1 for axis in range(len(extent))])
    return gain


def rank_bounds(count, lean):
    loads = [(1 << 20) // math.isqrt(rank ** lean) + 1 for rank in range(1, count + 1)]
    spread = 1 + sum(loads) // (1 << 30)
    return np.cumsum(np.array([max(1, weight // spread) for weight in loads]))


def skewed_ids(own_key, extent, amount, slope):
    grid = rank_bounds(amount, slope)
    pick = jax.random.randint(jax.random.fold_in(own_key, 1), extent, 0, int(grid[amount - 1]))
    rank = jnp.searchsorted(jnp.asarray(grid, jnp.int32), pick, side="right")
    return jax.random.permutation(jax.random.fold_in(own_key, 2), amount)[rank].astype(jnp.int32)


def scatter_about(own_key, shape, scale, bound, split=(), kind=jnp.bfloat16):
    array = jax.random.normal(own_key, shape, jnp.float32) * scale
    if len(split) > 0:
        array = block_scale(own_key, shape, split, -0.22, 0.18) * array
    return jnp.clip(array, min=-bound, max=bound).astype(kind)


def setup_inputs(seed: int = 0) -> dict:
    key_of = jax.random.split(jax.random.key(seed), 9)
    section_input = scatter_about(key_of[0], (N_PIPE, USERS, SEQ, D), 1.0, 6.0, ((0, 4), (1, 8), (2, 8)))
    event_ids = plant(skewed_ids(key_of[1], (USERS, SEQ), TYPES, 2), jax.random.fold_in(key_of[1], 3), 0, TYPES - 1).astype(jnp.int32)
    lengths = draw_lengths(jax.random.fold_in(key_of[8], 71), 0)
    clicks = plant((jax.random.randint(key_of[3], (USERS, SEQ), 0, 3) < 1).astype(jnp.int32), jax.random.fold_in(key_of[3], 1), 0, 1)
    conversions = plant((jax.random.randint(key_of[4], (USERS, SEQ), 0, 2) < 1).astype(jnp.int32), jax.random.fold_in(key_of[4], 1), 0, 1)
    conv_weight = scatter_about(key_of[5], (LAYERS, KERNEL * D, D), (KERNEL * D) ** -0.5, 0.109375, ((0, 4),))
    type_table = scatter_about(key_of[6], (LAYERS, TYPES, D), 0.5, 3.0, ((0, 4),))
    head_weight = scatter_about(key_of[7], (2, D), (D // 4) ** -0.5, 0.375)
    return {"section_input": section_input, "event_ids": event_ids, "lengths": lengths, "clicks": clicks, "conversions": conversions, "conv_weight": conv_weight, "type_table": type_table, "head_weight": head_weight}


EPS = 1e-06

def head_grad(out_bf, head_weight, click, convert, valid):
    logits = jnp.dot(out_bf, head_weight.T, preferred_element_type=jnp.float32)
    label_y = click.astype(jnp.float32)
    label_z = label_y * convert.astype(jnp.float32)
    weight_m = valid.astype(jnp.float32)

    def event_loss(first, second):
        soft = jax.nn.softplus
        rest = jnp.log(jax.nn.sigmoid(-first) + jax.nn.sigmoid(first) * jax.nn.sigmoid(-second))
        return label_y * soft(-first) + (1.0 - label_y) * soft(first) + label_z * (soft(-first) + soft(-second)) - (1.0 - label_z) * rest
    _, pull = jax.vjp(event_loss, logits[:, 0], logits[:, 1])
    grad_first, grad_second = pull(weight_m)
    grad_logits = jnp.stack([grad_first, grad_second], axis=1)
    return jnp.dot(grad_logits, head_weight.astype(jnp.float32), precision=lax.Precision.HIGHEST)

def delayed(values, steps):
    return jnp.concatenate([jnp.zeros((steps, values.shape[1]), values.dtype), values[:values.shape[0] - steps]], axis=0)

def advanced(values, steps):
    return jnp.concatenate([values[steps:], jnp.zeros((steps, values.shape[1]), values.dtype)], axis=0)

def reference(section_input, event_ids, lengths, clicks, conversions, conv_weight, type_table, head_weight):
    conv_list = []
    type_list = []
    grad_list = []
    incoming = None
    for section in reversed(range(LAYERS)):
        spacing = S_DEV // (4 * 2 ** section)
        weight = conv_weight[section]
        table = type_table[section]
        conv_total = jnp.zeros((KERNEL * D, D), jnp.float32)
        type_total = jnp.zeros((TYPES, D), jnp.float32)
        outgoing = []
        for user in range(USERS):
            inputs = section_input[section, user].astype(jnp.float32)
            inv_rms = lax.rsqrt(lax.optimization_barrier(jnp.mean(inputs * inputs, axis=-1, keepdims=True)) + EPS)
            normed = inputs * inv_rms
            normed_bf = normed.astype(jnp.bfloat16)
            taps = jnp.concatenate([delayed(normed_bf, tap * spacing) for tap in range(KERNEL)], axis=1)
            onehot = (event_ids[user][:, None] == jnp.arange(TYPES, dtype=jnp.int32)[None, :]).astype(jnp.bfloat16)
            pre = jnp.dot(taps, weight, preferred_element_type=jnp.float32) + jnp.dot(onehot, table, preferred_element_type=jnp.float32)
            if section == LAYERS - 1:
                out_bf = (inputs + jax.nn.gelu(pre)).astype(jnp.bfloat16)
                valid = jnp.arange(SEQ, dtype=jnp.int32) < lengths[user]
                grad_out = head_grad(out_bf, head_weight, clicks[user], conversions[user], valid)
            else:
                grad_out = incoming[user].astype(jnp.float32)
            _, pull = jax.vjp(jax.nn.gelu, pre)
            grad_pre = pull(grad_out)[0].astype(jnp.bfloat16)
            conv_total = conv_total + lax.dot_general(taps, grad_pre, (((0,), (0,)), ((), ())), preferred_element_type=jnp.float32)
            type_total = type_total + lax.dot_general(onehot, grad_pre, (((0,), (0,)), ((), ())), preferred_element_type=jnp.float32)
            grad_taps = lax.dot_general(grad_pre, weight, (((1,), (1,)), ((), ())), preferred_element_type=jnp.float32)
            grad_normed = grad_taps[:, :D]
            for tap in range(1, KERNEL):
                grad_normed = grad_normed + advanced(grad_taps[:, tap * D:(tap + 1) * D], tap * spacing)
            inner = lax.optimization_barrier(jnp.mean(grad_normed * normed, axis=-1, keepdims=True))
            grad_in = grad_out + inv_rms * (grad_normed - normed * inner)
            outgoing.append(grad_in.astype(jnp.bfloat16))
        incoming = outgoing
        conv_list.append(conv_total)
        type_list.append(type_total)
        grad_list.append(jnp.stack(outgoing, axis=0))
    conv_grad = jnp.stack(conv_list[::-1], axis=0)
    type_grad = jnp.stack(type_list[::-1], axis=0)
    input_grad = jnp.stack(grad_list[::-1], axis=0)
    return (conv_grad, type_grad, input_grad)
```

```python
import functools

import jax
import jax.numpy as jnp
from jax import lax
from jax.experimental import pallas as pl
from jax.experimental.pallas import tpu as pltpu
from jax.sharding import PartitionSpec as P

EPS = 1e-06
GELU_C = 0.7978845608028654
GELU_A = 0.044715
BF = jnp.bfloat16
F32 = jnp.float32
ROWS = 128
HALO = 64
EXT = ROWS + HALO
WIDTH = 1024
KERNEL = 3
KINDS = 64
GROUP = 8
OWN = KERNEL * WIDTH // (GROUP * GROUP)
CONV_ROWS = GROUP * OWN
SEND_ROWS = CONV_ROWS + 16
NT = (((1,), (1,)), ((), ()))


def spacing():
    return jnp.right_shift(jnp.int32(ROWS // 4), lax.axis_index("pipe"))


def rms_inv(x):
    return lax.rsqrt(jnp.mean(x * x, axis=-1, keepdims=True) + EPS)


def gelu_grad(x):
    x2 = x * x
    th = jnp.tanh(GELU_C * x * (1.0 + GELU_A * x2))
    slope = GELU_C * (1.0 + 3.0 * GELU_A * x2)
    value = 0.5 * x * (1.0 + th)
    grad = 0.5 * (1.0 + th) + 0.5 * x * (1.0 - th * th) * slope
    return value, grad


def shifted(base, sign, copy):
    d = spacing()
    is_last = lax.axis_index("pipe") == lax.axis_size("pipe") - 1
    least = ROWS // 4 >> (lax.axis_size("pipe") - 1)

    @pl.when(is_last)
    def _():
        for tap in range(KERNEL):
            copy(tap, base + sign * tap * least)

    @pl.when(jnp.logical_not(is_last))
    def _():
        for tap in range(KERNEL):
            copy(tap, pl.multiple_of(base + sign * tap * d, 8))


def input_side(g_ref, tap_ref, grad_out, x, w_ref):
    def copy(tap, start):
        tap_ref[tap, :ROWS] = g_ref[pl.ds(start, ROWS), :].astype(BF)

    shifted(0, 1, copy)
    grad_normed = None
    for tap in range(KERNEL):
        part = lax.dot_general(
            tap_ref[tap, :ROWS],
            w_ref[tap * WIDTH : (tap + 1) * WIDTH, :],
            NT,
            preferred_element_type=F32,
        )
        grad_normed = part if grad_normed is None else grad_normed + part
    inv = rms_inv(x)
    normed = x * inv
    inner = jnp.mean(grad_normed * normed, axis=-1, keepdims=True)
    return (grad_out + inv * (grad_normed - normed * inner)).astype(BF)


def first_kernel(
    len_ref, x_ref, prev_ref, own_ref, next_ref, w_ref, table_ref, head_ref,
    gp_ref, top_ref, gin_ref, edge_ref, normed_ref, g_ref, tap_ref,
):
    shard = lax.axis_index("seq")
    x_ext = jnp.concatenate(
        [prev_ref[...], x_ref[...], next_ref[:HALO, :]], axis=0
    ).astype(F32)
    normed_ref[...] = x_ext * rms_inv(x_ext)
    eye = (
        lax.broadcasted_iota(jnp.int32, (ROWS, ROWS), 0)
        == lax.broadcasted_iota(jnp.int32, (ROWS, ROWS), 1)
    ).astype(F32).astype(BF)
    meta = jnp.concatenate(
        [
            lax.dot_general(eye, ref[HALO:, :ROWS], NT, preferred_element_type=F32)
            for ref in (own_ref, next_ref)
        ],
        axis=0,
    )[:EXT]
    ids = meta[:, 0:1].astype(jnp.int32)
    label_y = meta[:, 1:2]
    label_z = label_y * meta[:, 2:3]
    onehot = (
        lax.broadcasted_iota(jnp.int32, (EXT, KINDS), 1) == ids
    ).astype(F32).astype(BF)
    def copy(tap, start):
        tap_ref[tap] = normed_ref[pl.ds(start, EXT), :].astype(BF)

    shifted(HALO, -1, copy)
    pre = jnp.dot(onehot, table_ref[...], preferred_element_type=F32)
    for tap in range(KERNEL):
        pre = pre + jnp.dot(
            tap_ref[tap],
            w_ref[tap * WIDTH : (tap + 1) * WIDTH, :],
            preferred_element_type=F32,
        )
    value, grad = gelu_grad(pre)
    gp_ref[...] = grad
    out = (x_ext[HALO:] + value).astype(BF).astype(F32)
    head = head_ref[...].astype(F32)
    first = jnp.sum(out * head[0:1], axis=-1, keepdims=True)
    second = jnp.sum(out * head[1:2], axis=-1, keepdims=True)
    a_pos, a_neg = jax.nn.sigmoid(first), jax.nn.sigmoid(-first)
    b_pos, b_neg = jax.nn.sigmoid(second), jax.nn.sigmoid(-second)
    rest = (1.0 - label_z) / (a_neg + a_pos * b_neg)
    grad_first = (
        (1.0 - label_y) * a_pos
        - (label_y + label_z) * a_neg
        + rest * (a_pos * a_neg * b_pos)
    )
    grad_second = rest * (a_pos * b_pos * b_neg) - label_z * b_neg
    position = shard * ROWS + lax.broadcasted_iota(jnp.int32, (EXT, 1), 0)
    valid = position < len_ref[0]
    grad_first = jnp.where(valid, grad_first, 0.0)
    grad_second = jnp.where(valid, grad_second, 0.0)
    top = grad_first * head[0:1] + grad_second * head[1:2]
    top_ref[...] = top

    g_ref[...] = top * grad
    gin = input_side(g_ref, tap_ref, top[:ROWS], x_ext[HALO : HALO + ROWS], w_ref)
    gin_ref[...] = gin
    edge_ref[...] = gin[: edge_ref.shape[0]]


def merged(main_ref, halo_ref, top_ref):
    is_last = lax.axis_index("pipe") == lax.axis_size("pipe") - 1
    halo = halo_ref[...].astype(F32)
    if halo.shape[0] < HALO:
        halo = jnp.concatenate([halo, jnp.zeros((HALO - halo.shape[0], WIDTH), F32)], axis=0)
    incoming = jnp.concatenate([main_ref[...].astype(F32), halo], axis=0)
    return jnp.where(is_last, top_ref[...], incoming)


def tick_kernel(main_ref, halo_ref, top_ref, gp_ref, x_ref, w_ref, gin_ref, edge_ref, g_ref, tap_ref):
    grad_out = merged(main_ref, halo_ref, top_ref)
    g_ref[...] = grad_out * gp_ref[...]
    gin = input_side(g_ref, tap_ref, grad_out[:ROWS], x_ref[...].astype(F32), w_ref)
    gin_ref[...] = gin
    edge_ref[...] = gin[: edge_ref.shape[0]]


def pack_kernel(main_ref, halo_ref, top_ref, gp_ref, ids_ref, g_ref):
    g = (merged(main_ref, halo_ref, top_ref) * gp_ref[...]).astype(BF)
    ids = ids_ref[...].astype(F32).astype(BF)
    for block in range(GROUP):
        g_ref[block, :EXT] = g[:, block * ROWS : (block + 1) * ROWS]
        g_ref[block, EXT:] = jnp.broadcast_to(ids, (16, ROWS))


def last_kernel(main_ref, halo_ref, top_ref, gp_ref, x_ref, w_ref, gin_ref, g_ref, tap_ref):
    grad_out = merged(main_ref, halo_ref, top_ref)
    g_ref[...] = grad_out * gp_ref[...]
    gin_ref[...] = input_side(g_ref, tap_ref, grad_out[:ROWS], x_ref[...].astype(F32), w_ref)


def normed_kernel(*refs):
    out_ref = refs[-1]
    for place, ref in enumerate(refs[:-1]):
        x = ref[...].astype(F32)
        out_ref[:, place * ROWS : (place + 1) * ROWS] = (x * rms_inv(x)).T.astype(BF)


def weight_kernel(offsets, g_ref, nt_ref, out_ref, wide_ref, rhs_ref, hot_ref):
    me = lax.axis_index("dp")
    wide_ref[...] = g_ref[...].astype(F32)
    line = lax.broadcasted_iota(jnp.int32, (ROWS, ROWS), 0)
    kind = jnp.where(line % 16 < GROUP, GROUP * (line % 16) + line // 16, -1).astype(F32)

    def copy(tap, start):
        for place, offset in enumerate(offsets):
            user = lax.rem(me + offset, GROUP)
            rhs_ref[place * ROWS : (place + 1) * ROWS, tap * ROWS : (tap + 1) * ROWS] = (
                wide_ref[user, pl.ds(start, ROWS), :].astype(BF)
            )

    shifted(0, 1, copy)
    for place, offset in enumerate(offsets):
        ids = wide_ref[lax.rem(me + offset, GROUP), EXT : EXT + 1, :]
        hot_ref[:, place * ROWS : (place + 1) * ROWS] = (kind == ids).astype(F32).astype(BF)
    conv = jnp.dot(nt_ref[...], rhs_ref[...], preferred_element_type=F32).astype(BF)
    kinds = jnp.dot(hot_ref[...], rhs_ref[:, :ROWS], preferred_element_type=F32).astype(BF)
    for group in range(GROUP):
        for shard in range(GROUP):
            row = (group * GROUP + shard) * OWN
            for piece in range(OWN // 16):
                tap, feature = divmod(row + piece * 16, WIDTH)
                out_ref[shard, group * OWN + piece * 16 : group * OWN + (piece + 1) * 16] = conv[
                    feature : feature + 16, tap * ROWS : (tap + 1) * ROWS
                ]
    for shard in range(GROUP):
        out_ref[shard, CONV_ROWS:] = kinds[shard * 16 : (shard + 1) * 16]


def sum_kernel(in_ref, out_ref):
    total = in_ref[0].astype(F32)
    for source in range(1, GROUP):
        total = total + in_ref[source].astype(F32)
    for group in range(GROUP):
        out_ref[group, :OWN] = total[group * OWN : (group + 1) * OWN].astype(BF)
        out_ref[group, OWN:] = jnp.broadcast_to(
            total[CONV_ROWS + group : CONV_ROWS + group + 1], (16, ROWS)
        ).astype(BF)


def place_kernel(in_ref, conv_ref, kind_ref):
    for block in range(GROUP):
        lanes = slice(block * ROWS, (block + 1) * ROWS)
        conv_ref[:, lanes] = in_ref[block, :OWN].astype(F32)
        kind_ref[:, lanes] = in_ref[block, OWN : OWN + 1].astype(F32)


def whole(space=pltpu.VMEM):
    return pl.BlockSpec(memory_space=space)


def call(kernel, outs, args, scratch=(), limit=24, first_smem=False, name=None):
    specs = [whole() for _ in args]
    if first_smem:
        specs[0] = whole(pltpu.SMEM)
    many = isinstance(outs, (list, tuple))
    return pl.pallas_call(
        kernel,
        out_shape=outs,
        in_specs=specs,
        out_specs=[whole() for _ in outs] if many else whole(),
        scratch_shapes=list(scratch),
        compiler_params=pltpu.CompilerParams(vmem_limit_bytes=limit << 20),
        name=name,
    )(*args)


def shaped(shape, dtype):
    return jax.ShapeDtypeStruct(shape, dtype)


def on_device(
    section_input, event_ids, lengths, clicks, conversions, conv_weight, type_table, head_weight
):
    x = section_input[0, 0]
    weight = conv_weight[0]
    table = type_table[0]
    shards = lax.axis_size("seq")
    sections = lax.axis_size("pipe")
    users = lax.axis_size("dp")

    meta = jnp.concatenate([event_ids, clicks, conversions], axis=0).astype(BF)
    own = jnp.concatenate([x[:HALO], jnp.pad(meta, ((0, 13), (0, WIDTH - ROWS)))], axis=0)
    following = lax.ppermute(own, "seq", [(i + 1, i) for i in range(shards - 1)])
    preceding = lax.ppermute(x[ROWS - HALO :], "seq", [(i, i + 1) for i in range(shards - 1)])

    def around(array, by):
        return lax.ppermute(array, "dp", [(i, (i + by) % users) for i in range(users)])

    def to_previous(array):
        return lax.ppermute(
            array, "pipe", [(i, i - 1) for i in range(1, sections)]
        )

    def to_previous_corner(array):
        pairs = [
            (p * shards + s, (p - 1) * shards + s - 1)
            for p in range(1, sections)
            for s in range(1, shards)
        ]
        return lax.ppermute(array, ("pipe", "seq"), pairs)

    wide = shaped((EXT, WIDTH), F32)
    narrow = shaped((ROWS, WIDTH), BF)
    scratch_g = pltpu.VMEM((EXT, WIDTH), F32)
    scratch_tap = pltpu.VMEM((KERNEL, EXT, WIDTH), BF)
    gp, top, gin, edge = call(
        first_kernel,
        [wide, wide, narrow, shaped((16, WIDTH), BF)],
        (lengths, x, preceding, own, following, weight, table, head_weight),
        [pltpu.VMEM((EXT + HALO, WIDTH), F32), scratch_g, scratch_tap],
        first_smem=True,
        name="first",
    )
    forward, backward = x, x
    blocks, offsets = [x], [0]
    for tick in range(1, sections):
        main = to_previous(gin)
        halo = to_previous_corner(edge)
        forward, backward = around(forward, 1), around(backward, -1)
        blocks += [forward, backward]
        offsets += [users - tick, tick]
        if tick + 1 < sections:
            gin, edge = call(
                tick_kernel,
                [narrow, shaped((16 << tick, WIDTH), BF)],
                (main, halo, top, gp, x, weight),
                [scratch_g, scratch_tap],
                name="tick",
            )
    blocks.append(around(forward, 1))
    offsets.append(users // 2)
    normed_t = call(
        normed_kernel, shaped((WIDTH, users * ROWS), BF), tuple(blocks), name="normed"
    )
    packed = call(
        pack_kernel, shaped((GROUP, EXT + 16, ROWS), BF), (main, halo, top, gp, event_ids), name="pack"
    )
    spread = lax.all_to_all(packed, "dp", 0, 0, tiled=True)
    gin = call(
        last_kernel, narrow, (main, halo, top, gp, x, weight), [scratch_g, scratch_tap], name="last"
    )
    partial = call(
        functools.partial(weight_kernel, tuple(offsets)),
        shaped((GROUP, SEND_ROWS, ROWS), BF),
        (spread, normed_t),
        [
            pltpu.VMEM((GROUP, EXT + 16, ROWS), F32),
            pltpu.VMEM((GROUP * ROWS, KERNEL * ROWS), BF),
            pltpu.VMEM((ROWS, GROUP * ROWS), BF),
        ],
        name="weight",
    )
    gathered = lax.all_to_all(partial, "seq", 0, 0, tiled=True)
    summed = call(sum_kernel, shaped((GROUP, HALO, ROWS), BF), (gathered,), name="sum")
    final = lax.all_to_all(summed, "dp", 0, 0, tiled=True)
    conv_share, type_share = call(
        place_kernel,
        [shaped((OWN, WIDTH), F32), shaped((1, WIDTH), F32)],
        (final,),
        name="place",
    )
    return (conv_share[None], type_share[None], gin[None, None])


def solution(mesh):
    placed = (
        P("pipe", "dp", "seq", None),
        P("dp", "seq"),
        P("dp"),
        P("dp", "seq"),
        P("dp", "seq"),
        P("pipe", None, None),
        P("pipe", None, None),
        P(),
    )
    return jax.shard_map(
        on_device,
        mesh=mesh,
        in_specs=placed,
        out_specs=(
            P("pipe", ("dp", "seq"), None),
            P("pipe", ("dp", "seq"), None),
            P("pipe", "dp", "seq", None),
        ),
        check_vma=False,
    )
```
